32 devices in a mesh: seq: 8 (over y, x, core), head: 4 (over z).
Axes of the slice: x: 2, y: 2, z: 4, core: 2. Of those that a mesh axis runs over, the one named last changes fastest.
Arguments:
- query_rows: bfloat16 [4096, 2048], P('seq', 'head'), may hold values from -6 to 6
- key_rows: bfloat16 [4096, 128], P('seq'), may hold values from -6 to 6
- value_rows: bfloat16 [4096, 128], P('seq'), may hold values from -6 to 6
- output_grad: bfloat16 [4096, 2048], P('seq', 'head'), may hold values from -0.59765625 to 0.59765625
- log_norm: float32 [16, 4096], P('head', 'seq'), may hold values from 0.5 to 3
- row_delta: float32 [16, 4096], P('head', 'seq'), may hold values from -5 to 5
- dispatch: int32 [8, 64], replicated, may hold values from 0 to 7, as said below
- listed_spans: int32 [8, 16], replicated, may hold values from 0 to 127, as said below
- range_start: int32 [8, 64], replicated, may hold values from 0 to 4088, as said below
Outputs:
- query_grad: bfloat16 [4096, 2048], P('seq', 'head')
- key_grad: float32 [128, 4096], P('head', 'seq')
- value_grad: float32 [128, 4096], P('head', 'seq')
The draws below stay inside these ranges and needn't reach their ends.
Inputs may be any that keep to these rules, and one draw needn't show every extreme that they name: `dispatch`: entry [h, j] names the group of query span 64 * h + j. Every group holds exactly 64 spans, and each row gives at most 8 spans to any one group, a number that every row reaches. `listed_spans`: row g holds 16 distinct key spans for group g. At most 2 of them lie among the 16 key spans of one index of seq, and every row reaches that number. `range_start`: entry [h, j] is at most 8 * (64 * h + j).
All inputs are finite; a program needn't handle non-finite values.
Results may differ from the reference program's by a relative error of at most 0.0046.
Values may be sent and summed in bfloat16 or wider, within the bound.
A program may use at most 64 MiB of HBM per device.

```python
import math
import jax
import jax.numpy as jnp
from jax import lax

HD = 128
GROUP = 16
SPAN = 8
KVCH = 32
NLIST = 16
CH_DEV = 64
HQ = 16
KVH = 1
OWNERS = 8
KV_DEV = 16
TOKENS = 4096


def draw_dispatch(key, part):
    first, second, third = jax.random.split(jax.random.fold_in(key, 11), 3)
    groups = min(OWNERS, CH_DEV)
    shuffle = jax.random.permutation(first, OWNERS)
    offsets = jax.random.permutation(second, OWNERS)[:groups]
    rotate = jax.random.randint(third, (OWNERS,), 0, CH_DEV)
    homes = jnp.arange(OWNERS, dtype=jnp.int32)[:, None]
    picks = (jnp.arange(CH_DEV, dtype=jnp.int32)[None, :] + rotate[:, None]) % CH_DEV % groups
    return shuffle[(homes + offsets[picks]) % OWNERS].astype(jnp.int32)


def draw_listed_spans(key, part):
    first, second, third = jax.random.split(jax.random.fold_in(key, 23), 3)
    groups = min(OWNERS, NLIST)
    per_home = NLIST // groups
    homes = jax.vmap(lambda item: jax.random.permutation(item, OWNERS)[:groups])(jax.random.split(first, OWNERS))
    subs = jax.vmap(lambda item: jax.random.permutation(item, KV_DEV)[:per_home])(jax.random.split(second, OWNERS * groups))
    chosen = (homes[:, :, None] * KV_DEV + subs.reshape(OWNERS, groups, per_home)).reshape(OWNERS, NLIST)
    shuffles = jax.vmap(lambda item: jax.random.permutation(item, NLIST))(jax.random.split(third, OWNERS))
    return jnp.take_along_axis(chosen, shuffles, axis=1).astype(jnp.int32)


def draw_range_start(key, part):
    span_ids = jnp.arange(OWNERS * CH_DEV, dtype=jnp.int32).reshape(OWNERS, CH_DEV)
    reach = jax.random.randint(jax.random.fold_in(key, 37), (OWNERS, CH_DEV), SPAN, TOKENS + 1)
    return jnp.maximum(0, (span_ids + 1) * SPAN - reach).astype(jnp.int32)


def steps_of(stream_key, dims, cuts, low, top_value):
    loudness = 1.0
    for dim, shards_of in cuts:
        heights = jax.random.uniform(jax.random.fold_in(jax.random.fold_in(stream_key, 6), dim), (shards_of,), jnp.float32, low / len(cuts), top_value / len(cuts))
        loudness = loudness * jnp.repeat(jnp.exp(heights), dims[dim] // shards_of).reshape((-1,) + (1,) * (len(dims) - 1 - dim))
    return loudness


def noise(rng, dims, spread, most, pieces=(), held_as=jnp.bfloat16):
    entries = jax.random.normal(rng, dims, jnp.float32) * spread
    if len(pieces) > 0:
        entries = steps_of(rng, dims, pieces, -0.22, 0.18) * entries
    return jnp.clip(entries, min=-most, max=most).astype(held_as)


def setup_inputs(seed: int = 0) -> dict:
    seeds = jax.random.split(jax.random.key(seed), 10)
    return {
        "query_rows": noise(seeds[0], (TOKENS, HQ * HD), 1.0, 6.0, ((0, 8), (1, 4))),
        "key_rows": noise(seeds[1], (TOKENS, KVH * HD), 1.0, 6.0, ((0, 8),)),
        "value_rows": noise(seeds[2], (TOKENS, KVH * HD), 1.0, 6.0, ((0, 8),)),
        "output_grad": noise(seeds[3], (TOKENS, HQ * HD), 0.09, 0.59765625, ((0, 8), (1, 4))),
        "log_norm": jnp.clip(0.5 + 2.5 * jax.random.uniform(seeds[4], (HQ, TOKENS), jnp.float32) ** steps_of(seeds[4], (HQ, TOKENS), ((0, 4), (1, 8)), -0.2, 0.2), 0.5, 3.0),
        "row_delta": noise(seeds[5], (HQ, TOKENS), 1.0, 5.0, ((0, 4), (1, 8)), jnp.float32),
        "dispatch": draw_dispatch(jax.random.fold_in(seeds[9], 71), 0),
        "listed_spans": draw_listed_spans(jax.random.fold_in(seeds[9], 71), 0),
        "range_start": draw_range_start(jax.random.fold_in(seeds[9], 71), 0),
    }


def reference(query_rows, key_rows, value_rows, output_grad, log_norm, row_delta, dispatch, listed_spans, range_start):
    owners = dispatch.shape[0]
    spans = dispatch.shape[1]
    score_scale = 1.0 / math.sqrt(HD)
    order = jnp.argsort(dispatch.reshape(-1), stable=True).astype(jnp.int32).reshape(owners, spans)
    starts = range_start.reshape(-1)
    query_all = query_rows.reshape(TOKENS, KVH, GROUP, HD)
    grad_all = output_grad.reshape(TOKENS, KVH, GROUP, HD)
    key_all = key_rows.reshape(TOKENS, KVH, HD)
    value_all = value_rows.reshape(TOKENS, KVH, HD)
    norm_all = log_norm.reshape(KVH, GROUP, TOKENS)
    delta_all = row_delta.reshape(KVH, GROUP, TOKENS)
    span_offsets = jnp.arange(SPAN, dtype=jnp.int32)
    block_offsets = jnp.arange(KVCH, dtype=jnp.int32)

    def one_owner(carry, owner):
        key_acc, value_acc = carry
        query_ids = order[owner]
        query_pos = (query_ids[:, None] * SPAN + span_offsets[None, :]).reshape(-1)
        key_pos = (listed_spans[owner][:, None] * KVCH + block_offsets[None, :]).reshape(-1)
        lowest = jnp.repeat(starts[query_ids], SPAN)
        allowed = (key_pos[None, :] <= query_pos[:, None]) & (key_pos[None, :] >= lowest[:, None])
        q_part = query_all[query_pos].astype(jnp.float32)
        g_part = grad_all[query_pos].astype(jnp.float32)
        k_part = key_all[key_pos].astype(jnp.float32)
        v_part = value_all[key_pos].astype(jnp.float32)
        scores = jnp.einsum('qagd,kad->agqk', q_part, k_part) * score_scale
        norms = norm_all[:, :, query_pos]
        deltas = delta_all[:, :, query_pos]
        probs = jnp.where(allowed[None, None], jnp.exp(scores - norms[..., None]), jnp.float32(0.0))
        dprobs = jnp.einsum('qagd,kad->agqk', g_part, v_part)
        dscores = probs * (dprobs - deltas[..., None])
        probs_round = lax.optimization_barrier(probs.astype(jnp.bfloat16)).astype(jnp.float32)
        dscores_round = lax.optimization_barrier(dscores.astype(jnp.bfloat16)).astype(jnp.float32)
        value_part = jnp.einsum('agqk,qagd->kad', probs_round, g_part)
        key_part = jnp.einsum('agqk,qagd->kad', dscores_round, q_part) * score_scale
        query_part = jnp.einsum('agqk,kad->qagd', dscores_round, k_part) * score_scale
        key_acc = key_acc.at[key_pos].add(key_part.reshape(-1, KVH * HD))
        value_acc = value_acc.at[key_pos].add(value_part.reshape(-1, KVH * HD))
        return ((key_acc, value_acc), query_part.reshape(-1, HQ * HD).astype(jnp.bfloat16))
    start_acc = (jnp.zeros((TOKENS, KVH * HD), jnp.float32), jnp.zeros((TOKENS, KVH * HD), jnp.float32))
    (key_acc, value_acc), stacked = lax.scan(one_owner, start_acc, jnp.arange(owners, dtype=jnp.int32))
    all_pos = (order.reshape(-1)[:, None] * SPAN + span_offsets[None, :]).reshape(-1)
    query_grad = jnp.zeros((TOKENS, HQ * HD), jnp.bfloat16).at[all_pos].set(stacked.reshape(-1, HQ * HD))
    return (query_grad, key_acc.T, value_acc.T)
```

```python
import math

import jax
import jax.numpy as jnp
from jax import lax
from jax.experimental import pallas as pl
from jax.experimental.pallas import tpu as pltpu
from jax.sharding import PartitionSpec as P

HD = 128
GROUP = 16
HQ_DEV = 4
SPAN = 8
KVCH = 32
NLIST = 16


HIGH = lax.Precision.HIGHEST


def passed_along(value, axis, by):
    length = lax.axis_size(axis)
    pairs = [(i, i + by) for i in range(length) if 0 <= i + by < length]
    return lax.ppermute(value, axis, pairs)


def earlier_same(labels):
    count = labels.shape[-1]
    same = labels[..., :, None] == labels[..., None, :]
    before = jnp.arange(count)[:, None] > jnp.arange(count)[None, :]
    return jnp.sum(same & before, axis=-1)


def one_hot(index, count):
    return (index[..., None] == jnp.arange(count, dtype=jnp.int32)).astype(jnp.float32)


def group_total(stacked, members, position, from_after):
    share = stacked.shape[1] // members

    def block(index):
        return lax.dynamic_slice_in_dim(stacked, index * share, share, 1)

    running = block((position + 1) % members)
    for step in range(1, members):
        running = from_after(running) + block((position + 1 + step) % members)
    return running


def local(
    query_rows,
    key_rows,
    value_rows,
    output_grad,
    log_norm,
    row_delta,
    dispatch,
    listed_spans,
    range_start,
):
    owners = lax.axis_size("seq")
    home_index = lax.axis_index("seq")
    head_index = lax.axis_index("head")
    spans = dispatch.shape[1]
    slot_count = max(1, spans // owners)
    kv_count = max(1, NLIST // owners)
    tok_dev = query_rows.shape[0]
    width = query_rows.shape[1]
    heads = width // HD
    blocks = tok_dev // KVCH
    members = GROUP // heads
    position = head_index % members
    kv_head = head_index * heads // GROUP
    score_scale = 1.0 / math.sqrt(HD)
    rank_all = earlier_same(dispatch)
    slot_all = dispatch * slot_count + rank_all
    to_slot = one_hot(slot_all[home_index], owners * slot_count)
    to_slot_bf = to_slot.astype(jnp.bfloat16)
    pick_bf = to_slot.T.astype(jnp.bfloat16)
    pick_float = to_slot.T

    def send_rows(rows):
        return (
            jnp.dot(pick_bf, rows.reshape(spans, -1), preferred_element_type=jnp.float32)
            .astype(jnp.bfloat16)
            .reshape(owners, slot_count * SPAN, -1)
        )

    def send_stats(stats):
        placed = jnp.dot(pick_float, stats.T.reshape(spans, SPAN * heads), precision=HIGH)
        return placed.reshape(owners, slot_count * SPAN, heads)

    list_home = listed_spans // blocks
    list_sub = listed_spans % blocks
    list_rank = earlier_same(list_home)
    mine = (list_home == home_index).astype(jnp.float32)
    rank_hot = one_hot(list_rank, kv_count) * mine[..., None]
    sub_hot = one_hot(list_sub, blocks)
    select = jnp.einsum("nir,nim->nrm", rank_hot, sub_hot, precision=HIGH).reshape(
        owners * kv_count, blocks
    )
    select_bf = select.astype(jnp.bfloat16)
    key_head = lax.dynamic_slice_in_dim(key_rows, kv_head * HD, HD, 1)
    value_head = lax.dynamic_slice_in_dim(value_rows, kv_head * HD, HD, 1)

    def send_blocks(rows):
        placed = jnp.dot(
            select_bf, rows.reshape(blocks, KVCH * HD), preferred_element_type=jnp.float32
        )
        return placed.astype(jnp.bfloat16).reshape(owners, kv_count * KVCH, HD)

    query_got, grad_got, key_got, value_got = (
        lax.all_to_all(send_rows(query_rows), "seq", split_axis=0, concat_axis=0, tiled=True),
        lax.all_to_all(send_rows(output_grad), "seq", split_axis=0, concat_axis=0, tiled=True),
        lax.all_to_all(send_blocks(key_head), "seq", split_axis=0, concat_axis=0, tiled=True),
        lax.all_to_all(send_blocks(value_head), "seq", split_axis=0, concat_axis=0, tiled=True),
    )
    norm_got, delta_got = (
        lax.all_to_all(send_stats(log_norm), "seq", split_axis=0, concat_axis=0, tiled=True),
        lax.all_to_all(send_stats(row_delta), "seq", split_axis=0, concat_axis=0, tiled=True),
    )
    live = (dispatch == home_index).reshape(-1)
    placement = jnp.cumsum(live.astype(jnp.int32)) - 1
    taken = live[:, None] & (placement[:, None] == jnp.arange(spans, dtype=jnp.int32)[None, :])
    source_slot = (jnp.arange(owners, dtype=jnp.int32)[:, None] * slot_count + rank_all).reshape(-1)
    compact = jnp.dot(
        taken.astype(jnp.float32).T, one_hot(source_slot, owners * slot_count), precision=HIGH
    )
    compact_bf = compact.astype(jnp.bfloat16)
    compact_back = compact.T.astype(jnp.bfloat16)
    flat_ids = jnp.arange(owners * spans, dtype=jnp.int32)
    span_ids = jnp.sum(jnp.where(taken, flat_ids[:, None], 0), axis=0)
    span_starts = jnp.sum(jnp.where(taken, range_start.reshape(-1)[:, None], 0), axis=0)

    def gather_rows(got):
        rows = jnp.dot(
            compact_bf, got.reshape(owners * slot_count, -1), preferred_element_type=jnp.float32
        )
        return rows.astype(jnp.bfloat16).reshape(spans * SPAN, heads, HD)

    def gather_stats(got):
        rows = jnp.dot(compact, got.reshape(owners * slot_count, SPAN * heads), precision=HIGH)
        return rows.reshape(spans * SPAN, heads).T

    query_mine = gather_rows(query_got)
    grad_mine = gather_rows(grad_got)
    norm_mine = gather_stats(norm_got)
    delta_mine = gather_stats(delta_got)
    my_list = listed_spans[home_index]
    kv_compact = one_hot(
        list_home[home_index] * kv_count + list_rank[home_index], owners * kv_count
    )
    kv_compact_bf = kv_compact.astype(jnp.bfloat16)

    def gather_blocks(got):
        rows = jnp.dot(
            kv_compact_bf,
            got.reshape(owners * kv_count, KVCH * HD),
            preferred_element_type=jnp.float32,
        )
        return rows.astype(jnp.bfloat16).reshape(NLIST * KVCH, HD)

    key_mine = gather_blocks(key_got)
    value_mine = gather_blocks(value_got)
    query_pos = (span_ids[:, None] * SPAN + jnp.arange(SPAN, dtype=jnp.int32)[None, :]).reshape(-1)
    key_pos = (my_list[:, None] * KVCH + jnp.arange(KVCH, dtype=jnp.int32)[None, :]).reshape(-1)
    lowest = jnp.repeat(span_starts, SPAN)
    allowed = (key_pos[None, :] <= query_pos[:, None]) & (key_pos[None, :] >= lowest[:, None])
    scores = (
        jnp.einsum("qhd,kd->hqk", query_mine, key_mine, preferred_element_type=jnp.float32)
        * score_scale
    )
    probs = jnp.where(allowed[None], jnp.exp(scores - norm_mine[:, :, None]), 0.0)
    dprobs = jnp.einsum("qhd,kd->hqk", grad_mine, value_mine, preferred_element_type=jnp.float32)
    dscores = probs * (dprobs - delta_mine[:, :, None])
    probs_bf = probs.astype(jnp.bfloat16)
    dscores_bf = dscores.astype(jnp.bfloat16)
    value_part = jnp.einsum("hqk,qhd->kd", probs_bf, grad_mine, preferred_element_type=jnp.float32)
    key_part = (
        jnp.einsum("hqk,qhd->kd", dscores_bf, query_mine, preferred_element_type=jnp.float32)
        * score_scale
    )
    query_part = (
        jnp.einsum("hqk,kd->qhd", dscores_bf, key_mine, preferred_element_type=jnp.float32)
        * score_scale
    )
    query_round = query_part.astype(jnp.bfloat16)
    query_send = jnp.dot(
        compact_back, query_round.reshape(spans, SPAN * width), preferred_element_type=jnp.float32
    )
    query_send = query_send.astype(jnp.bfloat16).reshape(owners, slot_count * SPAN, width)
    query_back = lax.all_to_all(query_send, "seq", split_axis=0, concat_axis=0, tiled=True)
    query_rows_out = jnp.dot(
        to_slot_bf,
        query_back.reshape(owners * slot_count, SPAN * width),
        preferred_element_type=jnp.float32,
    )
    query_out = query_rows_out.reshape(tok_dev, width).astype(jnp.bfloat16)

    def send_partial(part):
        rows = jnp.dot(kv_compact.T, part.reshape(NLIST, KVCH * HD), precision=HIGH)
        return rows.reshape(owners, kv_count * KVCH, HD)

    key_back, value_back = (
        lax.all_to_all(send_partial(key_part), "seq", split_axis=0, concat_axis=0, tiled=True),
        lax.all_to_all(send_partial(value_part), "seq", split_axis=0, concat_axis=0, tiled=True),
    )

    def home_rows(got):
        rows = jnp.dot(select.T, got.reshape(owners * kv_count, KVCH * HD), precision=HIGH)
        return rows.reshape(tok_dev, HD).T

    def after_home(running):
        nearby = passed_along(running, "head", -1)
        wrapped = passed_along(running, "head", GROUP // HQ_DEV - 1)
        return jnp.where(position == members - 1, wrapped, nearby)

    summed = group_total(
        jnp.stack([home_rows(key_back), home_rows(value_back)]), members, position, after_home
    )
    return (query_out, summed[0], summed[1])


BF = jnp.bfloat16
F32 = jnp.float32
I32 = jnp.int32


def mm(a, b, ca=1, cb=0):
    return lax.dot_general(a, b, (((ca,), (cb,)), ((), ())), preferred_element_type=F32)


def iota(shape, dim):
    return lax.broadcasted_iota(I32, shape, dim)


def pieces(x, count):
    out = []
    for _ in range(count):
        part = x.astype(BF)
        out.append(part)
        x = x - part.astype(F32)
    return out


def peer_chip(chip, k, chips):
    out, bit = 0, 1
    while bit < chips:
        out = out + (((chip // bit) + (k // bit)) % 2) * bit
        bit *= 2
    return out


def fused_kernel(
    q_ref, k_ref, v_ref, g_ref, ln_ref, rd_ref, disp_ref, list_ref, start_ref,
    dq_ref, dk_ref, dv_ref,
    kv_buf, perm, spread, qs, gs, qst, gst, lnb, rdb, posb, lowb, kpos, dq_acc,
    keep, x_snd, x_rcv, c_snd, c_rcv, z_snd, z_rcv, f_snd, f_rcv,
    d_ss, d_rs, p_ss, p_rs, x_ss, x_rs, c_ss, c_rs, z_ss, z_rs, f_ss, f_rs,
):
    owners = lax.axis_size("seq")
    members = lax.axis_size("head")
    chips = owners // 2
    tok = q_ref.shape[0]
    heads = q_ref.shape[1] // HD
    spans = disp_ref.shape[1]
    slots = spans // owners
    rows = slots * SPAN
    kvc = NLIST // owners
    keys = kvc * KVCH
    blocks = tok // KVCH
    lanes = 2 * keys
    shard = HD // members
    scale = 1.0 / math.sqrt(HD)
    me = lax.axis_index("seq")
    z = lax.axis_index("head")
    core = me % 2
    other = 1 - core
    chip = me // 2
    partner = chip * 2 + other
    near = [None] + [peer_chip(chip, k, chips) * 2 + core for k in range(1, chips)]

    def remote(src, dst, ss, rs, seq, head):
        return pltpu.make_async_remote_copy(
            src_ref=src, dst_ref=dst, send_sem=ss, recv_sem=rs,
            device_id={"seq": seq, "head": head}, device_id_type=pl.DeviceIdType.MESH,
        )

    barrier = pltpu.get_barrier_semaphore()
    greet = [(partner, z)] + [(near[k], z) for k in range(1, chips)]
    greet += [(me, (z + j) % members) for j in range(1, members)]
    for seq, head in greet:
        pl.semaphore_signal(
            barrier, inc=1, device_id={"seq": seq, "head": head},
            device_id_type=pl.DeviceIdType.MESH,
        )

    listed = list_ref[...].astype(F32)

    def picks(home):
        low = (home * blocks).astype(F32)
        mine = (listed >= low) & (listed < low + blocks)
        out, last = [], None
        for r in range(kvc):
            ok = mine if last is None else mine & (listed > last)
            last = jnp.min(jnp.where(ok, listed, 1e9), axis=1, keepdims=True)
            out.append(last)
        return out

    def make_spread(home, slot):
        got = picks(home)
        ahead = iota((KVCH, tok), 1) - iota((KVCH, tok), 0)
        for g in range(owners):
            for r in range(kvc):
                at = ((got[r][g:g + 1, :] - (home * blocks).astype(F32)) * KVCH).astype(I32)
                hot = jnp.where(ahead == at, 1.0, 0.0).astype(BF)
                base = g * keys + r * KVCH
                spread[slot, base:base + KVCH, :] = hot

    make_spread(me, core)
    kv_buf[0, core, :, 0:HD] = mm(spread[core], k_ref[...]).astype(BF)
    kv_buf[0, core, :, HD:2 * HD] = mm(spread[core], v_ref[...]).astype(BF)
    pl.semaphore_wait(barrier, len(greet))

    mine0 = kv_buf.at[0, core]
    direct, forward = {}, {}
    for k in range(1, chips):
        direct[k] = remote(mine0, kv_buf.at[k, core], d_ss.at[k], d_rs.at[k], near[k], z)
        direct[k].start()
    forward[0] = remote(mine0, mine0, p_ss.at[0], p_rs.at[0], partner, z)
    forward[0].start()

    make_spread(partner, other)
    for k in range(chips):
        lane = iota((owners, lanes), 1)
        value = jnp.zeros((owners, lanes), I32)
        for c in range(2):
            for r, got in enumerate(picks(peer_chip(chip, k, chips) * 2 + c)):
                block = c * kvc + r
                inside = (lane >= block * KVCH) & (lane < (block + 1) * KVCH)
                value = jnp.where(inside, (got * KVCH).astype(I32) + lane - block * KVCH, value)
        for g in range(owners):
            kpos[k, g] = value[g:g + 1, :]

    def my_row(ref):
        at = iota((owners, spans), 0) == me
        return jnp.sum(jnp.where(at, ref[...].astype(F32), 0.0), axis=0, keepdims=True)

    groups = my_row(disp_ref)
    eye = iota((spans, spans), 0) == iota((spans, spans), 1)
    column = jnp.sum(jnp.where(eye, groups, 0.0), axis=1, keepdims=True)
    earlier = iota((spans, spans), 0) < iota((spans, spans), 1)
    rank = jnp.sum(jnp.where((column == groups) & earlier, 1.0, 0.0), axis=0, keepdims=True)
    dest = groups * slots + rank
    starts = my_row(start_ref)
    start_hi = jnp.floor(starts * (1.0 / 256.0))
    start_lo = starts - start_hi * 256.0
    fill = jnp.zeros((5, spans), F32)
    small = jnp.concatenate([dest, start_hi, start_lo, fill], axis=0).astype(BF)
    behind = iota((spans, tok), 1) - iota((spans, tok), 0) * SPAN
    expand = jnp.where((behind >= 0) & (behind < SPAN), 1.0, 0.0).astype(BF)
    wide = mm(small, expand)
    token = iota((1, tok), 1)
    span_of = jnp.floor((token.astype(F32) + 0.5) * (1.0 / SPAN))
    within = token.astype(F32) - span_of * SPAN
    target = (wide[0:1, :] * SPAN + within).astype(I32)
    perm[...] = jnp.where(iota((tok, tok), 0) == target, 1.0, 0.0).astype(BF)

    parts = pieces(ln_ref[...], 3) + pieces(rd_ref[...], 3)
    parts += [wide[1:3, :].astype(BF), span_of.astype(BF)]
    parts.append(jnp.zeros((1, tok), BF))
    stats = jnp.concatenate([p.astype(F32) for p in parts], axis=0).astype(BF)
    placed = mm(perm[...], stats, 1, 1)
    hq = heads
    norm = placed[:, 0:hq] + placed[:, hq:2 * hq] + placed[:, 2 * hq:3 * hq]
    delta = placed[:, 3 * hq:4 * hq] + placed[:, 4 * hq:5 * hq] + placed[:, 5 * hq:6 * hq]
    low = placed[:, 6 * hq:6 * hq + 1] * 256.0 + placed[:, 6 * hq + 1:6 * hq + 2]
    slot_row = iota((tok, 1), 0).astype(F32)
    slot_in = slot_row - jnp.floor((slot_row + 0.5) * (1.0 / SPAN)) * SPAN
    pos = (placed[:, 6 * hq + 2:6 * hq + 3] + (me * spans).astype(F32)) * SPAN + slot_in
    posb[...] = jnp.broadcast_to(pos.astype(I32), (tok, lanes)).reshape(owners, rows, lanes)
    lowb[...] = jnp.broadcast_to(low.astype(I32), (tok, lanes)).reshape(owners, rows, lanes)
    q_slot = mm(perm[...], q_ref[...]).astype(BF)
    g_slot = mm(perm[...], g_ref[...]).astype(BF)
    for g in range(owners):
        at = slice(g * rows, (g + 1) * rows)
        for h in range(heads):
            to = slice(h * rows, (h + 1) * rows)
            qs[g, to, :] = q_slot[at, h * HD:(h + 1) * HD]
            gs[g, to, :] = g_slot[at, h * HD:(h + 1) * HD]
            lnb[g, to, :] = jnp.broadcast_to(norm[at, h:h + 1], (rows, lanes))
            rdb[g, to, :] = jnp.broadcast_to(delta[at, h:h + 1], (rows, lanes))

    def transposes(g, carry):
        qst[g] = qs[g].T
        gst[g] = gs[g].T
        return carry

    lax.fori_loop(0, owners, transposes, 0)
    is_first = core == 0

    def compute(k):
        def group(g, carry):
            at = pl.ds(pl.multiple_of(g * keys, keys), keys)
            key = jnp.concatenate([kv_buf[k, 0, at, 0:HD], kv_buf[k, 1, at, 0:HD]], axis=0)
            val = jnp.concatenate(
                [kv_buf[k, 0, at, HD:2 * HD], kv_buf[k, 1, at, HD:2 * HD]], axis=0
            )
            where_key = kpos[k, g]
            allowed = (where_key <= posb[g]) & (where_key >= lowb[g])
            allowed = jnp.concatenate([allowed] * heads, axis=0)
            scores = mm(qs[g], key, 1, 1) * scale
            probs = jnp.where(allowed, jnp.exp(scores - lnb[g]), 0.0)
            dprobs = mm(gs[g], val, 1, 1)
            dscores = probs * (dprobs - rdb[g])
            probs_b = probs.astype(BF)
            dscores_b = dscores.astype(BF)
            dv = mm(gst[g], probs_b)
            dk = mm(qst[g], dscores_b)
            keep[k, g] = jnp.where(is_first, dk, dv)
            x_snd[k, g] = jnp.where(is_first, dv, dk).astype(BF)
            dq = mm(dscores_b, key)
            if k == 0:
                dq_acc[g] = dq
            else:
                dq_acc[g] += dq
            return carry

        lax.fori_loop(0, owners, group, 0, unroll=2)

    def pass_on(k):
        direct[k].wait_recv()
        block = kv_buf.at[k, core]
        forward[k] = remote(block, block, p_ss.at[k], p_rs.at[k], partner, z)
        forward[k].start()

    swap, onward = {}, {}

    def exchange(k):
        swap[k] = remote(x_snd.at[k], x_rcv.at[k], x_ss.at[k], x_rs.at[k], partner, z)
        swap[k].start()

    def send_home(k):
        swap[k].wait_recv()
        c_snd[k] = (keep[k] + x_rcv[k].astype(F32)).astype(BF)
        onward[k] = remote(c_snd.at[k], c_rcv.at[k], c_ss.at[k], c_rs.at[k], near[k], z)
        onward[k].start()

    forward[0].wait_recv()
    compute(0)
    exchange(0)
    for k in range(1, min(3, chips)):
        pass_on(k)
    for k in range(1, chips):
        if k >= 3:
            pass_on(k)
        forward[k].wait_recv()
        compute(k)
        exchange(k)
        if k > 1:
            send_home(k - 1)
    if chips > 1:
        send_home(chips - 1)

    pulled = []
    for h in range(heads):
        to = slice(h * rows, (h + 1) * rows)
        pulled.append(
            jnp.concatenate([(dq_acc[g, to, :] * scale).astype(BF) for g in range(owners)], axis=0)
        )
    dq_ref[...] = mm(perm[...], jnp.concatenate(pulled, axis=1), 0, 0).astype(BF)

    swap[0].wait_recv()
    total = keep[0] + x_rcv[0].astype(F32)
    for k in range(1, chips):
        onward[k].wait_recv()
        total = total + c_rcv[k].astype(F32)
    keep[0] = total
    z_snd[...] = total.astype(BF)
    around = []
    for j in range(1, members):
        to = (z + j) % members
        piece = z_snd.at[:, pl.ds(pl.multiple_of(to * shard, shard), shard), :]
        copy = remote(piece, z_rcv.at[j], z_ss.at[j], z_rs.at[j], me, to)
        copy.start()
        around.append((j, copy))
    block = keep[0, :, pl.ds(pl.multiple_of(z * shard, shard), shard), :]
    for j, copy in around:
        copy.wait_recv()
        block = block + z_rcv[j].astype(F32)
    block = block * jnp.where(is_first, scale, 1.0)
    done = []
    for c in range(2):
        packed = jnp.concatenate([block[g][:, c * keys:(c + 1) * keys] for g in range(owners)], axis=1)
        got = mm(jnp.concatenate(pieces(packed, 3), axis=0), spread[c])
        done.append(got[0:shard] + got[shard:2 * shard] + got[2 * shard:3 * shard])
    f_snd[...] = jnp.where(is_first, done[1], done[0])
    last = remote(f_snd, f_rcv, f_ss, f_rs, partner, z)
    last.start()
    own = jnp.where(is_first, done[0], done[1])
    last.wait_recv()
    theirs = f_rcv[...]
    dk_ref[...] = jnp.where(is_first, own, theirs)
    dv_ref[...] = jnp.where(is_first, theirs, own)
    for copy in list(direct.values()) + list(forward.values()) + list(swap.values()):
        copy.wait_send()
    for copy in list(onward.values()) + [copy for _, copy in around] + [last]:
        copy.wait_send()


def fused(query_rows, key_rows, value_rows, output_grad, log_norm, row_delta, dispatch, listed_spans, range_start):
    owners = lax.axis_size("seq")
    members = lax.axis_size("head")
    chips = owners // 2
    tok, width = query_rows.shape
    heads = width // HD
    rows = dispatch.shape[1] // owners * SPAN
    keys = NLIST // owners * KVCH
    lanes = 2 * keys
    shard = HD // members
    vm = pltpu.VMEM
    dma = pltpu.SemaphoreType.DMA
    scratch = [
        vm((chips, 2, owners * keys, 2 * HD), BF),
        vm((tok, tok), BF),
        vm((2, owners * keys, tok), BF),
        vm((owners, heads * rows, HD), BF),
        vm((owners, heads * rows, HD), BF),
        vm((owners, HD, heads * rows), BF),
        vm((owners, HD, heads * rows), BF),
        vm((owners, heads * rows, lanes), F32),
        vm((owners, heads * rows, lanes), F32),
        vm((owners, rows, lanes), I32),
        vm((owners, rows, lanes), I32),
        vm((chips, owners, 1, lanes), I32),
        vm((owners, heads * rows, HD), F32),
        vm((chips, owners, HD, lanes), F32),
        vm((chips, owners, HD, lanes), BF),
        vm((chips, owners, HD, lanes), BF),
        vm((chips, owners, HD, lanes), BF),
        vm((chips, owners, HD, lanes), BF),
        vm((owners, HD, lanes), BF),
        vm((members, owners, shard, lanes), BF),
        vm((shard, tok), F32),
        vm((shard, tok), F32),
        dma((chips,)), dma((chips,)), dma((chips,)), dma((chips,)),
        dma((chips,)), dma((chips,)), dma((chips,)), dma((chips,)),
        dma((members,)), dma((members,)), dma, dma,
    ]
    spec = pl.BlockSpec(memory_space=pltpu.VMEM)
    return pl.pallas_call(
        fused_kernel,
        out_shape=(
            jax.ShapeDtypeStruct((tok, width), BF),
            jax.ShapeDtypeStruct((shard, tok), F32),
            jax.ShapeDtypeStruct((shard, tok), F32),
        ),
        in_specs=[spec] * 9,
        out_specs=(spec, spec, spec),
        scratch_shapes=scratch,
        compiler_params=pltpu.CompilerParams(
            collective_id=0, has_side_effects=True, vmem_limit_bytes=56 * 1024 * 1024
        ),
    )(query_rows, key_rows, value_rows, output_grad, log_norm, row_delta, dispatch, listed_spans, range_start)


def step(*args):
    query_rows, key_rows, dispatch = args[0], args[1], args[6]
    owners = lax.axis_size("seq")
    members = lax.axis_size("head")
    heads = query_rows.shape[1] // HD
    dense = (
        owners % 2 == 0
        and owners & (owners - 1) == 0
        and NLIST % owners == 0
        and 2 * NLIST // owners * KVCH == HD
        and dispatch.shape[1] % owners == 0
        and key_rows.shape[1] == HD
        and members * heads == GROUP
    )
    return fused(*args) if dense else local(*args)


def solution(mesh):
    placed = (
        P("seq", "head"),
        P("seq", None),
        P("seq", None),
        P("seq", "head"),
        P("head", "seq"),
        P("head", "seq"),
        P(),
        P(),
        P(),
    )
    return jax.shard_map(
        step,
        mesh=mesh,
        in_specs=placed,
        out_specs=(P("seq", "head"), P("head", "seq"), P("head", "seq")),
        check_vma=False,
    )
```

```python
import math

import jax
import jax.numpy as jnp
from jax import lax
from jax.experimental import pallas as pl
from jax.experimental.pallas import tpu as pltpu
from jax.sharding import PartitionSpec as P

HD = 128
GROUP = 16
HQ_DEV = 4
SPAN = 8
KVCH = 32
NLIST = 16


HIGH = lax.Precision.HIGHEST


def passed_along(value, axis, by):
    length = lax.axis_size(axis)
    pairs = [(i, i + by) for i in range(length) if 0 <= i + by < length]
    return lax.ppermute(value, axis, pairs)


def earlier_same(labels):
    count = labels.shape[-1]
    same = labels[..., :, None] == labels[..., None, :]
    before = jnp.arange(count)[:, None] > jnp.arange(count)[None, :]
    return jnp.sum(same & before, axis=-1)


def one_hot(index, count):
    return (index[..., None] == jnp.arange(count, dtype=jnp.int32)).astype(jnp.float32)


def group_total(stacked, members, position, from_after):
    share = stacked.shape[1] // members

    def block(index):
        return lax.dynamic_slice_in_dim(stacked, index * share, share, 1)

    running = block((position + 1) % members)
    for step in range(1, members):
        running = from_after(running) + block((position + 1 + step) % members)
    return running


def local(
    query_rows,
    key_rows,
    value_rows,
    output_grad,
    log_norm,
    row_delta,
    dispatch,
    listed_spans,
    range_start,
):
    owners = lax.axis_size("seq")
    home_index = lax.axis_index("seq")
    head_index = lax.axis_index("head")
    spans = dispatch.shape[1]
    slot_count = max(1, spans // owners)
    kv_count = max(1, NLIST // owners)
    tok_dev = query_rows.shape[0]
    width = query_rows.shape[1]
    heads = width // HD
    blocks = tok_dev // KVCH
    members = GROUP // heads
    position = head_index % members
    kv_head = head_index * heads // GROUP
    score_scale = 1.0 / math.sqrt(HD)
    rank_all = earlier_same(dispatch)
    slot_all = dispatch * slot_count + rank_all
    to_slot = one_hot(slot_all[home_index], owners * slot_count)
    to_slot_bf = to_slot.astype(jnp.bfloat16)
    pick_bf = to_slot.T.astype(jnp.bfloat16)
    pick_float = to_slot.T

    def send_rows(rows):
        return (
            jnp.dot(pick_bf, rows.reshape(spans, -1), preferred_element_type=jnp.float32)
            .astype(jnp.bfloat16)
            .reshape(owners, slot_count * SPAN, -1)
        )

    def send_stats(stats):
        placed = jnp.dot(pick_float, stats.T.reshape(spans, SPAN * heads), precision=HIGH)
        return placed.reshape(owners, slot_count * SPAN, heads)

    list_home = listed_spans // blocks
    list_sub = listed_spans % blocks
    list_rank = earlier_same(list_home)
    mine = (list_home == home_index).astype(jnp.float32)
    rank_hot = one_hot(list_rank, kv_count) * mine[..., None]
    sub_hot = one_hot(list_sub, blocks)
    select = jnp.einsum("nir,nim->nrm", rank_hot, sub_hot, precision=HIGH).reshape(
        owners * kv_count, blocks
    )
    select_bf = select.astype(jnp.bfloat16)
    key_head = lax.dynamic_slice_in_dim(key_rows, kv_head * HD, HD, 1)
    value_head = lax.dynamic_slice_in_dim(value_rows, kv_head * HD, HD, 1)

    def send_blocks(rows):
        placed = jnp.dot(
            select_bf, rows.reshape(blocks, KVCH * HD), preferred_element_type=jnp.float32
        )
        return placed.astype(jnp.bfloat16).reshape(owners, kv_count * KVCH, HD)

    query_got, grad_got, key_got, value_got = (
        lax.all_to_all(send_rows(query_rows), "seq", split_axis=0, concat_axis=0, tiled=True),
        lax.all_to_all(send_rows(output_grad), "seq", split_axis=0, concat_axis=0, tiled=True),
        lax.all_to_all(send_blocks(key_head), "seq", split_axis=0, concat_axis=0, tiled=True),
        lax.all_to_all(send_blocks(value_head), "seq", split_axis=0, concat_axis=0, tiled=True),
    )
    norm_got, delta_got = (
        lax.all_to_all(send_stats(log_norm), "seq", split_axis=0, concat_axis=0, tiled=True),
        lax.all_to_all(send_stats(row_delta), "seq", split_axis=0, concat_axis=0, tiled=True),
    )
    live = (dispatch == home_index).reshape(-1)
    placement = jnp.cumsum(live.astype(jnp.int32)) - 1
    taken = live[:, None] & (placement[:, None] == jnp.arange(spans, dtype=jnp.int32)[None, :])
    source_slot = (jnp.arange(owners, dtype=jnp.int32)[:, None] * slot_count + rank_all).reshape(-1)
    compact = jnp.dot(
        taken.astype(jnp.float32).T, one_hot(source_slot, owners * slot_count), precision=HIGH
    )
    compact_bf = compact.astype(jnp.bfloat16)
    compact_back = compact.T.astype(jnp.bfloat16)
    flat_ids = jnp.arange(owners * spans, dtype=jnp.int32)
    span_ids = jnp.sum(jnp.where(taken, flat_ids[:, None], 0), axis=0)
    span_starts = jnp.sum(jnp.where(taken, range_start.reshape(-1)[:, None], 0), axis=0)

    def gather_rows(got):
        rows = jnp.dot(
            compact_bf, got.reshape(owners * slot_count, -1), preferred_element_type=jnp.float32
        )
        return rows.astype(jnp.bfloat16).reshape(spans * SPAN, heads, HD)

    def gather_stats(got):
        rows = jnp.dot(compact, got.reshape(owners * slot_count, SPAN * heads), precision=HIGH)
        return rows.reshape(spans * SPAN, heads).T

    query_mine = gather_rows(query_got)
    grad_mine = gather_rows(grad_got)
    norm_mine = gather_stats(norm_got)
    delta_mine = gather_stats(delta_got)
    my_list = listed_spans[home_index]
    kv_compact = one_hot(
        list_home[home_index] * kv_count + list_rank[home_index], owners * kv_count
    )
    kv_compact_bf = kv_compact.astype(jnp.bfloat16)

    def gather_blocks(got):
        rows = jnp.dot(
            kv_compact_bf,
            got.reshape(owners * kv_count, KVCH * HD),
            preferred_element_type=jnp.float32,
        )
        return rows.astype(jnp.bfloat16).reshape(NLIST * KVCH, HD)

    key_mine = gather_blocks(key_got)
    value_mine = gather_blocks(value_got)
    query_pos = (span_ids[:, None] * SPAN + jnp.arange(SPAN, dtype=jnp.int32)[None, :]).reshape(-1)
    key_pos = (my_list[:, None] * KVCH + jnp.arange(KVCH, dtype=jnp.int32)[None, :]).reshape(-1)
    lowest = jnp.repeat(span_starts, SPAN)
    allowed = (key_pos[None, :] <= query_pos[:, None]) & (key_pos[None, :] >= lowest[:, None])
    scores = (
        jnp.einsum("qhd,kd->hqk", query_mine, key_mine, preferred_element_type=jnp.float32)
        * score_scale
    )
    probs = jnp.where(allowed[None], jnp.exp(scores - norm_mine[:, :, None]), 0.0)
    dprobs = jnp.einsum("qhd,kd->hqk", grad_mine, value_mine, preferred_element_type=jnp.float32)
    dscores = probs * (dprobs - delta_mine[:, :, None])
    probs_bf = probs.astype(jnp.bfloat16)
    dscores_bf = dscores.astype(jnp.bfloat16)
    value_part = jnp.einsum("hqk,qhd->kd", probs_bf, grad_mine, preferred_element_type=jnp.float32)
    key_part = (
        jnp.einsum("hqk,qhd->kd", dscores_bf, query_mine, preferred_element_type=jnp.float32)
        * score_scale
    )
    query_part = (
        jnp.einsum("hqk,kd->qhd", dscores_bf, key_mine, preferred_element_type=jnp.float32)
        * score_scale
    )
    query_round = query_part.astype(jnp.bfloat16)
    query_send = jnp.dot(
        compact_back, query_round.reshape(spans, SPAN * width), preferred_element_type=jnp.float32
    )
    query_send = query_send.astype(jnp.bfloat16).reshape(owners, slot_count * SPAN, width)
    query_back = lax.all_to_all(query_send, "seq", split_axis=0, concat_axis=0, tiled=True)
    query_rows_out = jnp.dot(
        to_slot_bf,
        query_back.reshape(owners * slot_count, SPAN * width),
        preferred_element_type=jnp.float32,
    )
    query_out = query_rows_out.reshape(tok_dev, width).astype(jnp.bfloat16)

    def send_partial(part):
        rows = jnp.dot(kv_compact.T, part.reshape(NLIST, KVCH * HD), precision=HIGH)
        return rows.reshape(owners, kv_count * KVCH, HD)

    key_back, value_back = (
        lax.all_to_all(send_partial(key_part), "seq", split_axis=0, concat_axis=0, tiled=True),
        lax.all_to_all(send_partial(value_part), "seq", split_axis=0, concat_axis=0, tiled=True),
    )

    def home_rows(got):
        rows = jnp.dot(select.T, got.reshape(owners * kv_count, KVCH * HD), precision=HIGH)
        return rows.reshape(tok_dev, HD).T

    def after_home(running):
        nearby = passed_along(running, "head", -1)
        wrapped = passed_along(running, "head", GROUP // HQ_DEV - 1)
        return jnp.where(position == members - 1, wrapped, nearby)

    summed = group_total(
        jnp.stack([home_rows(key_back), home_rows(value_back)]), members, position, after_home
    )
    return (query_out, summed[0], summed[1])


BF = jnp.bfloat16
F32 = jnp.float32
I32 = jnp.int32


CHUNKS = 2
CHIPS = 4
FIRST = 0


def mm(a, b, ca=1, cb=0):
    return lax.dot_general(a, b, (((ca,), (cb,)), ((), ())), preferred_element_type=F32)


def iota(shape, dim):
    return lax.broadcasted_iota(I32, shape, dim)


def pieces(x, count):
    out = []
    for _ in range(count):
        part = x.astype(BF)
        out.append(part)
        x = x - part.astype(F32)
    return out


def peer_chip(chip, k, chips):
    out, bit = 0, 1
    while bit < chips:
        out = out + (((chip // bit) + (k // bit)) % 2) * bit
        bit *= 2
    return out


def fused_kernel(
    q_ref, k_ref, v_ref, g_ref, ln_ref, rd_ref, disp_ref, list_ref, start_ref,
    dq_ref, dk_ref, dv_ref,
    kv_buf, perm, spread, qs, gs, qst, gst, lnb, rdb, posb, lowb, kpos, dq_acc,
    keep, x_snd, x_rcv, c_snd, c_rcv, z_snd, z_rcv, f_snd, f_rcv,
    q_in, g_in, dq_out,
    d_ss, d_rs, p_ss, p_rs, x_ss, x_rs, c_ss, c_rs, z_ss, z_rs, f_ss, f_rs, l_sem,
):
    owners = lax.axis_size("seq")
    members = lax.axis_size("head")
    chips = owners // 2
    tok = q_ref.shape[0]
    heads = q_ref.shape[1] // HD
    spans = disp_ref.shape[1]
    chunks = d_ss.shape[1]
    width = owners // chunks
    load_q = pltpu.make_async_copy(q_ref, q_in, l_sem.at[0])
    load_g = pltpu.make_async_copy(g_ref, g_in, l_sem.at[1])
    load_q.start()
    load_g.start()
    slots = spans // owners
    rows = slots * SPAN
    kvc = NLIST // owners
    keys = kvc * KVCH
    blocks = tok // KVCH
    lanes = 2 * keys
    shard = HD // members
    scale = 1.0 / math.sqrt(HD)
    me = lax.axis_index("seq")
    z = lax.axis_index("head")
    core = me % 2
    other = 1 - core
    chip = me // 2
    partner = chip * 2 + other
    near = [None] + [peer_chip(chip, k, chips) * 2 + core for k in range(1, chips)]

    def remote(src, dst, ss, rs, seq, head):
        return pltpu.make_async_remote_copy(
            src_ref=src, dst_ref=dst, send_sem=ss, recv_sem=rs,
            device_id={"seq": seq, "head": head}, device_id_type=pl.DeviceIdType.MESH,
        )

    barrier = pltpu.get_barrier_semaphore()
    greet = [(partner, z)] + [(near[k], z) for k in range(1, chips)]
    greet += [(me, (z + j) % members) for j in range(1, members)]
    for seq, head in greet:
        pl.semaphore_signal(
            barrier, inc=1, device_id={"seq": seq, "head": head},
            device_id_type=pl.DeviceIdType.MESH,
        )

    listed = list_ref[...].astype(F32)

    def picks(home):
        low = (home * blocks).astype(F32)
        mine = (listed >= low) & (listed < low + blocks)
        out, last = [], None
        for r in range(kvc):
            ok = mine if last is None else mine & (listed > last)
            last = jnp.min(jnp.where(ok, listed, 1e9), axis=1, keepdims=True)
            out.append(last)
        return out

    def make_spread(home, slot):
        got = picks(home)
        ahead = iota((KVCH, tok), 1) - iota((KVCH, tok), 0)
        for g in range(owners):
            for r in range(kvc):
                at = ((got[r][g:g + 1, :] - (home * blocks).astype(F32)) * KVCH).astype(I32)
                hot = jnp.where(ahead == at, 1.0, 0.0).astype(BF)
                base = g * keys + r * KVCH
                spread[slot, base:base + KVCH, :] = hot

    make_spread(me, core)
    kv_buf[0, core, :, 0:HD] = mm(spread[core], k_ref[...]).astype(BF)
    kv_buf[0, core, :, HD:2 * HD] = mm(spread[core], v_ref[...]).astype(BF)
    pl.semaphore_wait(barrier, len(greet))

    direct, forward, across = {}, {}, {}
    beside = z + 1 - 2 * (z % 2)

    def turn(c):
        return (c + z) % chunks

    def part(k, c):
        at = pl.multiple_of(turn(c) * width * keys, width * keys)
        return kv_buf.at[k, core, pl.ds(at, width * keys)]

    def to_partner(k, c):
        at = (k, turn(c))
        forward[k, c] = remote(part(k, c), part(k, c), p_ss.at[at], p_rs.at[at], partner, z)
        forward[k, c].start()

    for k in range(1, chips):
        at = (k, turn(0))
        direct[k] = remote(part(0, 0), part(k, 0), d_ss.at[at], d_rs.at[at], near[k], z)
        direct[k].start()
    for c in range(chunks):
        to_partner(0, c)

    make_spread(partner, other)
    for k in range(chips):
        lane = iota((owners, lanes), 1)
        value = jnp.zeros((owners, lanes), I32)
        for c in range(2):
            for r, got in enumerate(picks(peer_chip(chip, k, chips) * 2 + c)):
                block = c * kvc + r
                inside = (lane >= block * KVCH) & (lane < (block + 1) * KVCH)
                value = jnp.where(inside, (got * KVCH).astype(I32) + lane - block * KVCH, value)
        for g in range(owners):
            kpos[k, g] = value[g:g + 1, :]

    def my_row(ref):
        at = iota((owners, spans), 0) == me
        return jnp.sum(jnp.where(at, ref[...].astype(F32), 0.0), axis=0, keepdims=True)

    groups = my_row(disp_ref)
    eye = iota((spans, spans), 0) == iota((spans, spans), 1)
    column = jnp.sum(jnp.where(eye, groups, 0.0), axis=1, keepdims=True)
    earlier = iota((spans, spans), 0) < iota((spans, spans), 1)
    rank = jnp.sum(jnp.where((column == groups) & earlier, 1.0, 0.0), axis=0, keepdims=True)
    dest = groups * slots + rank
    starts = my_row(start_ref)
    start_hi = jnp.floor(starts * (1.0 / 256.0))
    start_lo = starts - start_hi * 256.0
    fill = jnp.zeros((5, spans), F32)
    small = jnp.concatenate([dest, start_hi, start_lo, fill], axis=0).astype(BF)
    behind = iota((spans, tok), 1) - iota((spans, tok), 0) * SPAN
    expand = jnp.where((behind >= 0) & (behind < SPAN), 1.0, 0.0).astype(BF)
    wide = mm(small, expand)
    token = iota((1, tok), 1)
    span_of = jnp.floor((token.astype(F32) + 0.5) * (1.0 / SPAN))
    within = token.astype(F32) - span_of * SPAN
    target = (wide[0:1, :] * SPAN + within).astype(I32)
    perm[...] = jnp.where(iota((tok, tok), 0) == target, 1.0, 0.0).astype(BF)

    parts = pieces(ln_ref[...], 3) + pieces(rd_ref[...], 3)
    parts += [wide[1:3, :].astype(BF), span_of.astype(BF)]
    parts.append(jnp.zeros((1, tok), BF))
    stats = jnp.concatenate([p.astype(F32) for p in parts], axis=0).astype(BF)
    placed = mm(perm[...], stats, 1, 1)
    hq = heads
    norm = placed[:, 0:hq] + placed[:, hq:2 * hq] + placed[:, 2 * hq:3 * hq]
    delta = placed[:, 3 * hq:4 * hq] + placed[:, 4 * hq:5 * hq] + placed[:, 5 * hq:6 * hq]
    low = placed[:, 6 * hq:6 * hq + 1] * 256.0 + placed[:, 6 * hq + 1:6 * hq + 2]
    slot_row = iota((tok, 1), 0).astype(F32)
    slot_in = slot_row - jnp.floor((slot_row + 0.5) * (1.0 / SPAN)) * SPAN
    pos = (placed[:, 6 * hq + 2:6 * hq + 3] + (me * spans).astype(F32)) * SPAN + slot_in
    posb[...] = jnp.broadcast_to(pos.astype(I32), (tok, lanes)).reshape(owners, rows, lanes)
    lowb[...] = jnp.broadcast_to(low.astype(I32), (tok, lanes)).reshape(owners, rows, lanes)
    load_q.wait()
    q_slot = mm(perm[...], q_in[...]).astype(BF)
    load_g.wait()
    g_slot = mm(perm[...], g_in[...]).astype(BF)
    for g in range(owners):
        at = slice(g * rows, (g + 1) * rows)
        for h in range(heads):
            to = slice(h * rows, (h + 1) * rows)
            qs[g, to, :] = q_slot[at, h * HD:(h + 1) * HD]
            gs[g, to, :] = g_slot[at, h * HD:(h + 1) * HD]
            lnb[g, to, :] = jnp.broadcast_to(norm[at, h:h + 1], (rows, lanes))
            rdb[g, to, :] = jnp.broadcast_to(delta[at, h:h + 1], (rows, lanes))

    def transposes(g, carry):
        qst[g] = qs[g].T
        gst[g] = gs[g].T
        return carry

    lax.fori_loop(0, owners, transposes, 0)
    is_first = core == 0

    def compute(k, c):
        def group(i, carry):
            g = turn(c) * width + i
            at = pl.ds(pl.multiple_of(g * keys, keys), keys)
            key = jnp.concatenate([kv_buf[k, 0, at, 0:HD], kv_buf[k, 1, at, 0:HD]], axis=0)
            val = jnp.concatenate(
                [kv_buf[k, 0, at, HD:2 * HD], kv_buf[k, 1, at, HD:2 * HD]], axis=0
            )
            where_key = kpos[k, g]
            allowed = (where_key <= posb[g]) & (where_key >= lowb[g])
            allowed = jnp.concatenate([allowed] * heads, axis=0)
            scores = mm(qs[g], key, 1, 1) * scale
            probs = jnp.where(allowed, jnp.exp(scores - lnb[g]), 0.0)
            dprobs = mm(gs[g], val, 1, 1)
            dscores = probs * (dprobs - rdb[g])
            probs_b = probs.astype(BF)
            dscores_b = dscores.astype(BF)
            dv = mm(gst[g], probs_b)
            dk = mm(qst[g], dscores_b)
            keep[k, g] = jnp.where(is_first, dk, dv)
            x_snd[k, g] = jnp.where(is_first, dv, dk).astype(BF)
            dq = mm(dscores_b, key)
            if k == FIRST:
                dq_acc[g] = dq
            else:
                dq_acc[g] += dq
            return carry

        lax.fori_loop(0, width, group, 0, unroll=min(width, 4))
        exchange(k, c)

    swap, onward, around = {}, {}, {}

    def those(c):
        return pl.ds(turn(c) * width, width)

    def exchange(k, c):
        swap[k, c] = remote(
            x_snd.at[k, those(c)], x_rcv.at[k, those(c)], x_ss.at[k, turn(c)], x_rs.at[k, turn(c)], partner, z
        )
        swap[k, c].start()

    def send_home(k, c):
        swap[k, c].wait_recv()
        c_snd[k, those(c)] = (keep[k, those(c)] + x_rcv[k, those(c)].astype(F32)).astype(BF)
        onward[k, c] = remote(
            c_snd.at[k, those(c)], c_rcv.at[k, those(c)], c_ss.at[k, turn(c)], c_rs.at[k, turn(c)], near[k], z
        )
        onward[k, c].start()

    def pass_first(k):
        direct[k].wait_recv()
        across[k] = remote(
            part(k, 0), part(k, 0), d_ss.at[k, turn(1)], d_rs.at[k, turn(0)], me, beside
        )
        across[k].start()
        to_partner(k, 0)

    def pass_second(k):
        remote(
            part(k, 1), part(k, 1), d_ss.at[k, turn(1)], d_rs.at[k, turn(1)], me, beside
        ).wait_recv()
        to_partner(k, 1)

    def work(k, c):
        forward[k, c].wait_recv()
        compute(k, c)

    def total_up(c):
        swap[0, c].wait_recv()
        total = keep[0, those(c)] + x_rcv[0, those(c)].astype(F32)
        for k in range(1, chips):
            onward[k, c].wait_recv()
            total = total + c_rcv[k, those(c)].astype(F32)
        keep[0, those(c)] = total
        z_snd[those(c)] = total.astype(BF)
        for j in range(1, members):
            to = (z + j) % members
            piece = z_snd.at[those(c), pl.ds(pl.multiple_of(to * shard, shard), shard), :]
            around[j, c] = remote(
                piece, z_rcv.at[j, those(c)], z_ss.at[j, turn(c)], z_rs.at[j, turn(c)], me, to
            )
            around[j, c].start()

    done = [None, None]

    def settle(c):
        block = keep[0, those(c), pl.ds(pl.multiple_of(z * shard, shard), shard), :]
        for j in range(1, members):
            around[j, c].wait_recv()
            block = block + z_rcv[j, those(c)].astype(F32)
        block = block * jnp.where(is_first, scale, 1.0)
        base = pl.multiple_of(turn(c) * width * keys, width * keys)
        for side in range(2):
            packed = jnp.concatenate(
                [block[i][:, side * keys:(side + 1) * keys] for i in range(width)], axis=1
            )
            hot = spread[side, pl.ds(base, width * keys), :]
            got = mm(jnp.concatenate(pieces(packed, 2), axis=0), hot)
            got = got[0:shard] + got[shard:2 * shard]
            done[side] = got if done[side] is None else done[side] + got

    work(0, 0)
    pass_first(1)
    pass_first(2)
    work(1, 0)
    pass_first(3)
    work(2, 0)
    send_home(1, 0)
    work(3, 0)
    send_home(2, 0)
    pass_second(1)
    work(0, 1)
    send_home(3, 0)
    work(1, 1)
    pass_second(2)
    send_home(1, 1)
    work(2, 1)
    pass_second(3)
    send_home(2, 1)
    work(3, 1)
    send_home(chips - 1, 1)
    pulled = []
    for h in range(heads):
        to = slice(h * rows, (h + 1) * rows)
        pulled.append(
            jnp.concatenate([(dq_acc[g, to, :] * scale).astype(BF) for g in range(owners)], axis=0)
        )
    dq_out[...] = mm(perm[...], jnp.concatenate(pulled, axis=1), 0, 0).astype(BF)
    save = pltpu.make_async_copy(dq_out, dq_ref, l_sem.at[2])
    save.start()
    total_up(0)
    total_up(1)
    for c in range(chunks):
        settle(c)
    f_snd[...] = jnp.where(is_first, done[1], done[0])
    last = remote(f_snd, f_rcv, f_ss, f_rs, partner, z)
    last.start()
    own = jnp.where(is_first, done[0], done[1])
    last.wait_recv()
    theirs = f_rcv[...]
    dk_ref[...] = jnp.where(is_first, own, theirs)
    dv_ref[...] = jnp.where(is_first, theirs, own)
    for made in (direct, forward, across, swap, onward, around):
        for copy in made.values():
            copy.wait_send()
    last.wait_send()
    save.wait()


def place_kernel(a_ref, b_ref, c_ref, x_ref, y_ref, w_ref, sems):
    pairs = ((a_ref, x_ref), (b_ref, y_ref), (c_ref, w_ref))
    moves = [pltpu.make_async_copy(a, b, sems.at[i]) for i, (a, b) in enumerate(pairs)]
    for move in moves:
        move.start()
    for move in moves:
        move.wait()


def place(outs):
    spec = pl.BlockSpec(memory_space=pltpu.VMEM)
    far = pl.BlockSpec(memory_space=pl.ANY)
    return pl.pallas_call(
        place_kernel,
        out_shape=tuple(jax.ShapeDtypeStruct(o.shape, o.dtype) for o in outs),
        in_specs=[spec] * 3,
        out_specs=(far,) * 3,
        scratch_shapes=[pltpu.SemaphoreType.DMA((3,))],
    )(*outs)


def fused(query_rows, key_rows, value_rows, output_grad, log_norm, row_delta, dispatch, listed_spans, range_start):
    owners = lax.axis_size("seq")
    members = lax.axis_size("head")
    chips = owners // 2
    tok, width = query_rows.shape
    heads = width // HD
    rows = dispatch.shape[1] // owners * SPAN
    keys = NLIST // owners * KVCH
    lanes = 2 * keys
    shard = HD // members
    chunks = CHUNKS
    vm = pltpu.VMEM
    dma = pltpu.SemaphoreType.DMA
    scratch = [
        vm((chips, 2, owners * keys, 2 * HD), BF),
        vm((tok, tok), BF),
        vm((2, owners * keys, tok), BF),
        vm((owners, heads * rows, HD), BF),
        vm((owners, heads * rows, HD), BF),
        vm((owners, HD, heads * rows), BF),
        vm((owners, HD, heads * rows), BF),
        vm((owners, heads * rows, lanes), F32),
        vm((owners, heads * rows, lanes), F32),
        vm((owners, rows, lanes), I32),
        vm((owners, rows, lanes), I32),
        vm((chips, owners, 1, lanes), I32),
        vm((owners, heads * rows, HD), F32),
        vm((chips, owners, HD, lanes), F32),
        vm((chips, owners, HD, lanes), BF),
        vm((chips, owners, HD, lanes), BF),
        vm((chips, owners, HD, lanes), BF),
        vm((chips, owners, HD, lanes), BF),
        vm((owners, HD, lanes), BF),
        vm((members, owners, shard, lanes), BF),
        vm((shard, tok), F32),
        vm((shard, tok), F32),
        vm((tok, width), BF),
        vm((tok, width), BF),
        vm((tok, width), BF),
        dma((chips, chunks)), dma((chips, chunks)), dma((chips, chunks)), dma((chips, chunks)),
        dma((chips, chunks)), dma((chips, chunks)), dma((chips, chunks)), dma((chips, chunks)),
        dma((members, chunks)), dma((members, chunks)), dma, dma, dma((3,)),
    ]
    spec = pl.BlockSpec(memory_space=pltpu.VMEM)
    far = pl.BlockSpec(memory_space=pl.ANY)
    return pl.pallas_call(
        fused_kernel,
        out_shape=(
            jax.ShapeDtypeStruct((tok, width), BF),
            jax.ShapeDtypeStruct((shard, tok), F32),
            jax.ShapeDtypeStruct((shard, tok), F32),
        ),
        in_specs=[far, spec, spec, far] + [spec] * 5,
        out_specs=(far, spec, spec),
        scratch_shapes=scratch,
        compiler_params=pltpu.CompilerParams(
            collective_id=0, has_side_effects=True, vmem_limit_bytes=56 * 1024 * 1024
        ),
    )(query_rows, key_rows, value_rows, output_grad, log_norm, row_delta, dispatch, listed_spans, range_start)


def step(*args):
    query_rows, key_rows, dispatch = args[0], args[1], args[6]
    owners = lax.axis_size("seq")
    members = lax.axis_size("head")
    heads = query_rows.shape[1] // HD
    dense = (
        owners // 2 == CHIPS
        and members % CHUNKS == 0
        and NLIST % owners == 0
        and 2 * NLIST // owners * KVCH == HD
        and dispatch.shape[1] % owners == 0
        and key_rows.shape[1] == HD
        and members * heads == GROUP
    )
    return place(fused(*args)) if dense else local(*args)


def solution(mesh):
    placed = (
        P("seq", "head"),
        P("seq", None),
        P("seq", None),
        P("seq", "head"),
        P("head", "seq"),
        P("head", "seq"),
        P(),
        P(),
        P(),
    )
    return jax.shard_map(
        step,
        mesh=mesh,
        in_specs=placed,
        out_specs=(P("seq", "head"), P("head", "seq"), P("head", "seq")),
        check_vma=False,
    )
```
